32 devices in a mesh: doc: 8 (over y, x, core), seq: 4 (over z).
Axes of the slice: x: 2, y: 2, z: 4, core: 2. Of those that a mesh axis runs over, the one named last changes fastest.
Arguments:
- images: bfloat16 [8, 4, 128, 8192], P('doc', None, None, 'seq'), may hold values from -6 to 6
- kv_weight: bfloat16 [1024, 8192], P('doc', 'seq'), may hold values from -0.0625 to 0.0625
- q_gain: float32 [128], replicated, may hold values from 0.1 to 1.9
- k_gain: float32 [128], replicated, may hold values from 0.1 to 1.9
- queries: bfloat16 [8, 512, 4096], P('doc', 'seq'), may hold values from -6 to 6
- cotangent: bfloat16 [8, 512, 4096], P('doc', 'seq'), may hold values from -6 to 6
- tile_count: int32 [8], replicated, may hold values from 1 to 4, as said below
- tile_target: int32 [8, 4], replicated, may hold values from 0 to 8, as said below
- tile_source: int32 [8, 4], replicated, may hold values from 0 to 8, as said below
- text_length: int32 [8], replicated, may hold values from 64 to 512, as said below
Outputs:
- attn_out: bfloat16 [8, 512, 4096], P('doc', 'seq')
- kv_weight_grad: float32 [1024, 8192], P('doc', 'seq')
The draws below stay inside these ranges and needn't reach their ends.
Inputs may be any that keep to these rules, and one draw needn't show every extreme that they name: `tile_count`: some document has 4 tiles and some has 1. `tile_target`: 8 marks an empty slot. The tile in slot k of an encoder device is tile k of its document; no encoder device holds two tiles of one document. Agrees with tile_source and tile_count. `tile_source`: 8 for k at or beyond the document's tile count; otherwise the encoder device that holds tile k in its slot k. `text_length`: live rows come first; some document has all 512 rows live.
All inputs are finite; a program needn't handle non-finite values.
Results may differ from the reference program's by a relative error of at most 0.03.
Values may be sent and summed in bfloat16 or wider, within the bound.
No kernel may reach another device: no remote copies, remote signals or barrier semaphores. Data moves between devices by JAX's collectives and lax.ppermute only.
A program may use at most 64 MiB of HBM per device.

```python
import math
import jax
import jax.numpy as jnp
from jax import lax

D = 8192
HQ = 32
HD = 128
SLOTS = 4
TT = 128
TOK_DEV = 128
KVW = 512
TEXT = 512
DOCS = 8
N_DOC = 8
N_SEQ = 4


def routing_tables(key):
    base = jax.random.fold_in(key, 7)
    first, second, third, fourth, fifth, sixth = jax.random.split(base, 6)
    counts = jax.random.randint(first, (DOCS,), 1, SLOTS + 1)
    order = jax.random.permutation(second, DOCS)
    counts = counts.at[order[0]].set(SLOTS).at[order[1]].set(1)
    outer = jax.random.permutation(third, N_DOC)
    inner = jax.random.permutation(fourth, DOCS)
    slot_ids = jnp.arange(SLOTS)
    sources = outer[(inner[:, None] + slot_ids[None, :]) % N_DOC]
    sources = jnp.where(slot_ids[None, :] < counts[:, None], sources, N_DOC)
    outer_inv = jnp.argsort(outer)
    inner_inv = jnp.argsort(inner)
    doc_of = inner_inv[(outer_inv[:, None] - slot_ids[None, :]) % N_DOC]
    targets = jnp.where(slot_ids[None, :] < counts[doc_of], doc_of, DOCS)
    lengths = jax.random.randint(fifth, (DOCS,), TEXT // 8, TEXT + 1)
    longest = jax.random.randint(sixth, (), 0, DOCS)
    lengths = lengths.at[longest].set(TEXT)
    return (counts.astype(jnp.int32), targets.astype(jnp.int32), sources.astype(jnp.int32), lengths.astype(jnp.int32))


def draw_tile_count(key, part):
    return routing_tables(key)[0]


def draw_tile_target(key, part):
    return routing_tables(key)[1]


def draw_tile_source(key, part):
    return routing_tables(key)[2]


def draw_text_length(key, part):
    return routing_tables(key)[3]


def block_scale(own_key, extent, shards, least, high):
    def one(axis_at, shards_of):
        steps = jax.random.uniform(jax.random.fold_in(jax.random.fold_in(own_key, 6), axis_at), (shards_of,), jnp.float32, least / len(shards), high / len(shards))
        return jnp.repeat(jnp.exp(steps), extent[axis_at] // shards_of).reshape((-1,) + (1,) * (len(extent) - axis_at - 1))

    loudness = one(*shards[0])
    for cut in shards[1:]:
        loudness = loudness * one(*cut)
    return loudness


def scatter_about(stream_key, extent, scale, most, cuts=(), held_as=jnp.bfloat16):
    gain = block_scale(stream_key, extent, cuts, -0.22, 0.18) if cuts else 1.0
    result = jax.random.normal(stream_key, extent, jnp.float32) * scale * gain
    return jnp.minimum(jnp.maximum(result, -most), most).astype(held_as)


def setup_inputs(seed: int = 0) -> dict:
    streams_of = jax.random.split(jax.random.key(seed), 11)
    return {
        "images": scatter_about(streams_of[0], (N_DOC, SLOTS, TT, D), 1.0, 6.0, ((0, 8), (3, 4))),
        "kv_weight": scatter_about(streams_of[1], (2 * KVW, D), D ** -0.5, 0.0625, ((0, 8), (1, 4))),
        "q_gain": jnp.clip(1.0 + 0.18 * jax.random.normal(streams_of[2], (HD,), jnp.float32), 0.1, 1.9),
        "k_gain": jnp.clip(1.0 + 0.18 * jax.random.normal(streams_of[3], (HD,), jnp.float32), 0.1, 1.9),
        "queries": scatter_about(streams_of[4], (DOCS, TEXT, HQ * HD), 1.0, 6.0, ((0, 8), (1, 4))),
        "cotangent": scatter_about(streams_of[5], (DOCS, TEXT, HQ * HD), 1.0, 6.0, ((0, 8), (1, 4))),
        "tile_count": draw_tile_count(jax.random.fold_in(streams_of[10], 71), 0),
        "tile_target": draw_tile_target(jax.random.fold_in(streams_of[10], 71), 0),
        "tile_source": draw_tile_source(jax.random.fold_in(streams_of[10], 71), 0),
        "text_length": draw_text_length(jax.random.fold_in(streams_of[10], 71), 0),
    }


EPS = 1e-05

def product(form, left, right):
    return jnp.einsum(form, left.astype(jnp.float32), right.astype(jnp.float32))

def cross_core(kv_tiles, query_rows, grad_rows, q_gain, k_gain, key_live, row_live):
    key_width = kv_tiles.shape[-1] // 2
    head_dim = q_gain.shape[0]
    kv_heads = key_width // head_dim
    token_rows = query_rows.shape[0]
    q_heads = query_rows.shape[1] // head_dim
    group_size = q_heads // kv_heads
    inv_root = 1.0 / math.sqrt(head_dim)
    key_raw = kv_tiles[:, :key_width].reshape(-1, kv_heads, head_dim).astype(jnp.float32)
    values = kv_tiles[:, key_width:].reshape(-1, kv_heads, head_dim)
    key_scale = lax.rsqrt(lax.optimization_barrier(jnp.mean(key_raw * key_raw, axis=-1, keepdims=True)) + EPS)
    key_normed = (key_raw * key_scale * k_gain).astype(jnp.bfloat16)
    query_raw = query_rows.reshape(token_rows, kv_heads, group_size, head_dim).astype(jnp.float32)
    query_scale = lax.rsqrt(lax.optimization_barrier(jnp.mean(query_raw * query_raw, axis=-1, keepdims=True)) + EPS)
    query_normed = (query_raw * query_scale * q_gain).astype(jnp.bfloat16)
    scores = product('tkgd,lkd->tkgl', query_normed, key_normed) * inv_root
    expd = jnp.exp(scores) * key_live
    attend = expd / lax.optimization_barrier(jnp.sum(expd, axis=-1, keepdims=True))
    attend_low = attend.astype(jnp.bfloat16)
    mixed = product('tkgl,lkd->tkgd', attend_low, values)
    row_mask = row_live[:, None, None, None]
    attn_rows = (mixed * row_mask).astype(jnp.bfloat16).reshape(token_rows, -1)
    grad_live = grad_rows.reshape(token_rows, kv_heads, group_size, head_dim) * row_mask.astype(jnp.bfloat16)
    grad_attend = product('tkgd,lkd->tkgl', grad_live, values)
    grad_scores = attend * (grad_attend - lax.optimization_barrier(jnp.sum(attend * grad_attend, axis=-1, keepdims=True)))
    grad_low = (grad_scores * inv_root).astype(jnp.bfloat16)
    grad_keyn = product('tkgl,tkgd->lkd', grad_low, query_normed)
    grad_values = product('tkgl,tkgd->lkd', attend_low, grad_live)
    weighted = grad_keyn * k_gain
    cubed = key_scale * key_scale * key_scale
    grad_keys = key_scale * weighted - key_raw * cubed * lax.optimization_barrier(jnp.mean(weighted * key_raw, axis=-1, keepdims=True))
    grad_kv = jnp.concatenate([grad_keys.reshape(-1, key_width), grad_values.reshape(-1, key_width)], axis=-1)
    return (attn_rows, grad_kv)

def reference(images, kv_weight, q_gain, k_gain, queries, cotangent, tile_count, tile_target, tile_source, text_length):
    width = kv_weight.shape[0]
    block_cols = D // N_SEQ
    flat = images.reshape(-1, D)
    image_blocks = jnp.moveaxis(flat.reshape(-1, N_SEQ, block_cols), 1, 0)
    weight_blocks = jnp.moveaxis(kv_weight.reshape(width, N_SEQ, block_cols), 1, 0)

    def add_block(total, items):
        image_part, weight_part = items
        term = jnp.dot(image_part, weight_part.T, preferred_element_type=jnp.float32).astype(jnp.bfloat16)
        return (total + term.astype(jnp.float32), None)
    kv_sum, unused = lax.scan(add_block, jnp.zeros((flat.shape[0], width), jnp.float32), (image_blocks, weight_blocks))
    kv_enc = kv_sum.astype(jnp.bfloat16).reshape(N_DOC, SLOTS, TT, width)
    slot_ids = jnp.arange(SLOTS, dtype=jnp.int32)
    source_safe = jnp.minimum(tile_source, N_DOC - 1).astype(jnp.int32)
    kv_doc = kv_enc[source_safe, slot_ids[None, :]]
    live_slot = slot_ids[None, :] < tile_count[:, None]
    kv_doc = jnp.where(live_slot[:, :, None, None], kv_doc, jnp.zeros((), jnp.bfloat16))

    def per_doc(items):
        kv_tiles, query_rows, grad_rows, count_doc, length_doc = items
        key_live = (jnp.arange(SLOTS * TT, dtype=jnp.int32) // TT < count_doc).astype(jnp.float32)
        kv_flat = kv_tiles.reshape(SLOTS * TT, width)
        shard_ids = jnp.arange(N_SEQ, dtype=jnp.int32)

        def per_shard(shard_items):
            shard_at, query_shard, grad_shard = shard_items
            row_index = shard_at * TOK_DEV + jnp.arange(TOK_DEV, dtype=jnp.int32)
            row_live = (row_index < length_doc).astype(jnp.float32)
            attn_rows, grad_kv = cross_core(kv_flat, query_shard, grad_shard, q_gain, k_gain, key_live, row_live)
            return (attn_rows, grad_kv.astype(jnp.bfloat16))
        query_shards = query_rows.reshape(N_SEQ, TOK_DEV, -1)
        grad_shards = grad_rows.reshape(N_SEQ, TOK_DEV, -1)
        attn_shards, grad_parts = lax.map(per_shard, (shard_ids, query_shards, grad_shards))
        grad_sum = lax.optimization_barrier(jnp.sum(grad_parts.astype(jnp.float32), axis=0))
        return (attn_shards.reshape(TEXT, -1), grad_sum.astype(jnp.bfloat16))
    attn_out, grad_doc = lax.map(per_doc, (kv_doc, queries, cotangent, tile_count, text_length))
    grad_doc = grad_doc.reshape(DOCS, SLOTS, TT, width)
    target_safe = jnp.minimum(tile_target, DOCS - 1).astype(jnp.int32)
    grad_enc = grad_doc[target_safe, slot_ids[None, :]]
    grad_enc = jnp.where((tile_target < DOCS)[:, :, None, None], grad_enc, jnp.zeros((), jnp.bfloat16))
    weight_grad = jnp.dot(grad_enc.reshape(-1, width).T, flat, preferred_element_type=jnp.float32)
    return (attn_out, weight_grad)
```

```python
import functools
import math

import jax
import jax.numpy as jnp
from jax import lax
from jax.experimental import pallas as pl
from jax.experimental.pallas import tpu as pltpu
from jax.sharding import PartitionSpec as P

EPS = 1e-05
LOG2E = 1.4426950408889634


def cross_core(kv_tiles, query_rows, grad_rows, q_gain, k_gain, key_live, row_live):
    key_width = kv_tiles.shape[-1] // 2
    head_dim = q_gain.shape[0]
    kv_heads = key_width // head_dim
    token_rows = query_rows.shape[0]
    q_heads = query_rows.shape[1] // head_dim
    group_size = q_heads // kv_heads
    inv_root = 1.0 / math.sqrt(head_dim)
    key_raw = kv_tiles[:, :key_width].reshape(-1, kv_heads, head_dim).astype(jnp.float32)
    values = kv_tiles[:, key_width:].reshape(-1, kv_heads, head_dim)
    key_scale = lax.rsqrt(jnp.mean(key_raw * key_raw, axis=-1, keepdims=True) + EPS)
    key_normed = (key_raw * key_scale * k_gain).astype(jnp.bfloat16)
    query_raw = query_rows.reshape(token_rows, kv_heads, group_size, head_dim).astype(jnp.float32)
    query_scale = lax.rsqrt(jnp.mean(query_raw * query_raw, axis=-1, keepdims=True) + EPS)
    query_normed = (query_raw * query_scale * q_gain).astype(jnp.bfloat16)
    row_mask = row_live[:, None, None, None]
    grad_live = grad_rows.reshape(token_rows, kv_heads, group_size, head_dim) * row_mask.astype(
        jnp.bfloat16
    )

    def one_head(items):
        key_head, value_head, query_head, grad_head = items
        scores = (
            jnp.einsum("tgd,ld->tgl", query_head, key_head, preferred_element_type=jnp.float32)
            * inv_root
        )
        expd = jnp.exp(scores) * key_live
        attend = expd / jnp.sum(expd, axis=-1, keepdims=True)
        attend_low = attend.astype(jnp.bfloat16)
        mixed = jnp.einsum(
            "tgl,ld->tgd", attend_low, value_head, preferred_element_type=jnp.float32
        )
        mixed_low = (mixed * row_live[:, None, None]).astype(jnp.bfloat16)
        grad_attend = jnp.einsum(
            "tgd,ld->tgl", grad_head, value_head, preferred_element_type=jnp.float32
        )
        grad_scores = attend * (grad_attend - jnp.sum(attend * grad_attend, axis=-1, keepdims=True))
        grad_low = (grad_scores * inv_root).astype(jnp.bfloat16)
        grad_keyn = jnp.einsum(
            "tgl,tgd->ld", grad_low, query_head, preferred_element_type=jnp.float32
        )
        grad_values = jnp.einsum(
            "tgl,tgd->ld", attend_low, grad_head, preferred_element_type=jnp.float32
        )
        return (mixed_low, grad_keyn, grad_values)

    head_items = (
        jnp.moveaxis(key_normed, 1, 0),
        jnp.moveaxis(values, 1, 0),
        jnp.moveaxis(query_normed, 1, 0),
        jnp.moveaxis(grad_live, 1, 0),
    )
    mixed_heads, keyn_heads, value_heads = lax.map(one_head, head_items)
    attn_rows = jnp.moveaxis(mixed_heads, 0, 1).reshape(token_rows, -1)
    grad_keyn = jnp.moveaxis(keyn_heads, 0, 1)
    grad_values = jnp.moveaxis(value_heads, 0, 1)
    weighted = grad_keyn * k_gain
    cubed = key_scale * key_scale * key_scale
    grad_keys = key_scale * weighted - key_raw * cubed * jnp.mean(
        weighted * key_raw, axis=-1, keepdims=True
    )
    grad_kv = jnp.concatenate(
        [grad_keys.reshape(-1, key_width), grad_values.reshape(-1, key_width)], axis=-1
    )
    return (attn_rows, grad_kv)


def any_mesh_device(
    images,
    kv_weight,
    q_gain,
    k_gain,
    queries,
    cotangent,
    tile_count,
    tile_target,
    tile_source,
    text_length,
):
    n_doc = lax.axis_size("doc")
    n_seq = lax.axis_size("seq")
    doc_at = lax.axis_index("doc")
    seq_at = lax.axis_index("seq")
    slots = images.shape[1]
    tile_rows = images.shape[2]
    part_rows = tile_rows // n_seq
    own_cols = images[0].reshape(slots * tile_rows, images.shape[3])
    partial_value = lax.dot_general(
        own_cols,
        lax.all_gather(kv_weight, "doc", axis=0, tiled=True),
        (((1,), (1,)), ((), ())),
        preferred_element_type=jnp.float32,
    )
    width = partial_value.shape[1]
    partial_value = partial_value.reshape(slots, tile_rows, width)
    summed = lax.psum(partial_value.astype(jnp.bfloat16), "seq").astype(jnp.float32)
    own_share = lax.dynamic_slice_in_dim(summed, seq_at * part_rows, part_rows, 1)
    kv_own = own_share.astype(jnp.bfloat16)
    doc_ids = jnp.arange(n_doc, dtype=jnp.int32)
    slot_ids = jnp.arange(slots, dtype=jnp.int32)
    targets = tile_target[doc_at]
    send_map = (targets[None, :] == doc_ids[:, None]).astype(jnp.bfloat16)
    outgoing = jnp.einsum(
        "ds,src->drc", send_map, kv_own, preferred_element_type=jnp.float32
    ).astype(jnp.bfloat16)
    incoming = lax.all_to_all(outgoing, "doc", split_axis=0, concat_axis=0, tiled=True)
    tiles_here = tile_count[doc_at]
    sources = tile_source[doc_at]
    live_slot = slot_ids < tiles_here
    pick_map = ((sources[:, None] == doc_ids[None, :]) & live_slot[:, None]).astype(jnp.bfloat16)
    kv_part = jnp.einsum(
        "se,erc->src", pick_map, incoming, preferred_element_type=jnp.float32
    ).astype(jnp.bfloat16)
    kv_full = lax.all_gather(kv_part, "seq", axis=1, tiled=True)
    token_rows = queries.shape[1]
    key_live = (jnp.arange(slots * tile_rows, dtype=jnp.int32) // tile_rows < tiles_here).astype(
        jnp.float32
    )
    row_index = seq_at * token_rows + jnp.arange(token_rows, dtype=jnp.int32)
    row_live = (row_index < text_length[doc_at]).astype(jnp.float32)
    attn_rows, grad_kv = cross_core(
        kv_full.reshape(slots * tile_rows, width),
        queries[0],
        cotangent[0],
        q_gain,
        k_gain,
        key_live,
        row_live,
    )
    attn_out = attn_rows[None]
    grad_kv = grad_kv.reshape(slots, tile_rows, width)
    grad_sum = lax.psum(grad_kv.astype(jnp.bfloat16), "seq").astype(jnp.float32)
    grad_share = lax.dynamic_slice_in_dim(grad_sum, seq_at * part_rows, part_rows, 1)
    grad_own = grad_share.astype(jnp.bfloat16)
    back_out = jnp.einsum(
        "se,src->erc", pick_map, grad_own, preferred_element_type=jnp.float32
    ).astype(jnp.bfloat16)
    back_in = lax.all_to_all(back_out, "doc", split_axis=0, concat_axis=0, tiled=True)
    returned = jnp.einsum(
        "ds,drc->src", send_map, back_in, preferred_element_type=jnp.float32
    ).astype(jnp.bfloat16)
    grad_full = lax.all_gather(returned, "seq", axis=1, tiled=True)
    grad_flat = grad_full.reshape(slots * tile_rows, width)
    rows_each = width // n_doc
    weight_part = lax.dot_general(
        grad_flat, own_cols, (((0,), (0,)), ((), ())), preferred_element_type=jnp.float32
    )
    weight_sum = lax.psum(weight_part.astype(jnp.bfloat16), "doc").astype(jnp.float32)
    weight_grad = lax.dynamic_slice_in_dim(weight_sum, doc_at * rows_each, rows_each, 0)
    return (attn_out, weight_grad)


def swap_doc(value, step):
    pairs = [(at, at ^ step) for at in range(lax.axis_size("doc"))]
    return lax.ppermute(value, "doc", pairs)


def swap_seq(value, step):
    pairs = [(at, at ^ step) for at in range(lax.axis_size("seq"))]
    return lax.ppermute(value, "seq", pairs)


def swap_some(value, doc_step, seq_step, keep):
    n_doc = lax.axis_size("doc")
    n_seq = lax.axis_size("seq")
    pairs = [
        (doc * n_seq + seq, (doc ^ doc_step) * n_seq + (seq ^ seq_step))
        for doc in range(n_doc)
        for seq in range(n_seq)
        if keep(doc, seq)
    ]
    return lax.ppermute(value, ("doc", "seq"), pairs)


def whole(shape):
    return pl.BlockSpec(shape, lambda *_: (0,) * len(shape))


def dispatch_kernel(tile, table_ref, *refs):
    first, second = refs[:4], refs[4:8]
    outs, both = refs[8:-1], refs[-1]
    width = first[0].shape[1]

    def total(parts):
        value = parts[0][...].astype(jnp.float32)
        for part in parts[1:]:
            value = value + part[...].astype(jnp.float32)
        return value.astype(jnp.bfloat16)

    keys_first = table_ref[0] == 0

    @pl.when(keys_first)
    def _():
        both[:, :width] = total(first)
        both[:, width:] = total(second)

    @pl.when(jnp.logical_not(keys_first))
    def _():
        both[:, :width] = total(second)
        both[:, width:] = total(first)

    for step, out in enumerate(outs):
        slot = table_ref[1 + step]
        out[...] = both[pl.ds(pl.multiple_of(slot * tile, tile), tile), :]


def dispatch(table, first, second, tile, n_doc):
    rows, width = first[0].shape
    return pl.pallas_call(
        functools.partial(dispatch_kernel, tile),
        grid_spec=pltpu.PrefetchScalarGridSpec(
            num_scalar_prefetch=1,
            grid=(1,),
            in_specs=[whole((rows, width))] * 8,
            out_specs=[whole((tile, 2 * width))] * n_doc,
            scratch_shapes=[pltpu.VMEM((rows, 2 * width), jnp.bfloat16)],
        ),
        out_shape=[jax.ShapeDtypeStruct((tile, 2 * width), jnp.bfloat16)] * n_doc,
        name="dispatch",
    )(table, *first, *second)


def attend_kernel(slots, steps, table_ref, *refs):
    tiles = refs[:8]
    queries, cotangents = refs[8:12], refs[12:16]
    q_gain, k_gain, row_live = refs[16:19]
    outs, grads = refs[19:23], refs[23:31]
    key_raw, key_norm, values, values_t, grad_k, grad_v = refs[31:]
    tile, head_dim = tiles[0].shape[0], key_raw.shape[1]
    inv_root = 1.0 / math.sqrt(head_dim)
    step = pl.program_id(0)
    count = table_ref[1]

    def slot_rows(slot):
        return slice(slot * tile, (slot + 1) * tile)

    @pl.when(step == 0)
    def _():
        for slot in range(slots):
            live = slot < count
            origin = table_ref[2 + slot]

            @pl.when(jnp.logical_not(live))
            def _():
                key_raw[slot_rows(slot), :] = jnp.zeros((tile, head_dim), jnp.bfloat16)
                values[slot_rows(slot), :] = jnp.zeros((tile, head_dim), jnp.bfloat16)

            for index in range(8):

                @pl.when(jnp.logical_and(live, origin == index))
                def _():
                    key_raw[slot_rows(slot), :] = tiles[index][:, :head_dim]
                    values[slot_rows(slot), :] = tiles[index][:, head_dim:]

        raw = key_raw[...].astype(jnp.float32)
        scale = lax.rsqrt(jnp.mean(raw * raw, axis=-1, keepdims=True) + EPS)
        key_norm[...] = (raw * scale * k_gain[...]).astype(jnp.bfloat16)
        values_t[...] = values[...].astype(jnp.float32).T.astype(jnp.bfloat16)
        grad_k[...] = jnp.zeros_like(grad_k)
        grad_v[...] = jnp.zeros_like(grad_v)

    for half in range(2):
        lanes = slice(2 * half * tile, 2 * (half + 1) * tile)
        raw = jnp.concatenate(
            [queries[2 * half][...], queries[2 * half + 1][...]], axis=0
        ).astype(jnp.float32)
        grad_in = jnp.concatenate([cotangents[2 * half][...], cotangents[2 * half + 1][...]], axis=0)
        scale = lax.rsqrt(jnp.mean(raw * raw, axis=-1, keepdims=True) + EPS)
        query = (raw * scale * q_gain[...]).astype(jnp.bfloat16)
        scores = lax.dot_general(
            key_norm[...], query, (((1,), (1,)), ((), ())), preferred_element_type=jnp.float32
        )
        expd = jnp.exp2(scores * (inv_root * LOG2E))
        total = jnp.zeros((1, expd.shape[1]), jnp.float32)
        for slot in range(slots):
            part = jnp.sum(expd[slot_rows(slot), :], axis=0, keepdims=True)
            total = total + jnp.where(slot < count, part, 0.0)
        attend = expd * (row_live[:, lanes] / total)
        attend_low = attend.astype(jnp.bfloat16)
        mixed = jnp.dot(values_t[...], attend_low, preferred_element_type=jnp.float32).T
        outs[2 * half][...] = mixed[:tile].astype(jnp.bfloat16)
        outs[2 * half + 1][...] = mixed[tile:].astype(jnp.bfloat16)
        grad_attend = lax.dot_general(
            values[...], grad_in, (((1,), (1,)), ((), ())), preferred_element_type=jnp.float32
        )
        product = attend * grad_attend
        shift = jnp.sum(product, axis=0, keepdims=True)
        grad_low = ((product - attend * shift) * inv_root).astype(jnp.bfloat16)
        grad_k[...] += jnp.dot(grad_low, query, preferred_element_type=jnp.float32)
        grad_v[...] += jnp.dot(attend_low, grad_in, preferred_element_type=jnp.float32)

    @pl.when(step == steps - 1)
    def _():
        raw = key_raw[...].astype(jnp.float32)
        scale = lax.rsqrt(jnp.mean(raw * raw, axis=-1, keepdims=True) + EPS)
        weighted = grad_k[...] * k_gain[...]
        cubed = scale * scale * scale
        grad_raw = scale * weighted - raw * cubed * jnp.mean(
            weighted * raw, axis=-1, keepdims=True
        )
        key_norm[...] = grad_raw.astype(jnp.bfloat16)
        values[...] = grad_v[...].astype(jnp.bfloat16)
        for grad in grads:
            grad[...] = jnp.zeros_like(grad)
        for slot in range(slots):
            live = slot < count
            origin = table_ref[2 + slot]
            for index in range(8):

                @pl.when(jnp.logical_and(live, origin == index))
                def _():
                    grads[index][:, :head_dim] = key_norm[slot_rows(slot), :]
                    grads[index][:, head_dim:] = values[slot_rows(slot), :]


def attend_call(table, tiles, own_query, queries, own_cotangent, cotangents, q_gain, k_gain, row_live, slots):
    tile, width = tiles[0].shape
    head_dim = width // 2
    tokens, group_width = queries[0].shape
    group = group_width // head_dim
    keys = slots * tile
    own = pl.BlockSpec((None, tokens, head_dim), lambda at, table: (0, 0, table[0] * group + at))
    moved = pl.BlockSpec((tokens, head_dim), lambda at, table: (0, at))
    return pl.pallas_call(
        functools.partial(attend_kernel, slots, group),
        grid_spec=pltpu.PrefetchScalarGridSpec(
            num_scalar_prefetch=1,
            grid=(group,),
            in_specs=[whole((tile, width))] * 8
            + [own] + [moved] * 3 + [own] + [moved] * 3
            + [whole((1, head_dim)), whole((1, head_dim)), whole((1, 4 * tokens))],
            out_specs=[moved] * 4 + [whole((tile, width))] * 8,
            scratch_shapes=[
                pltpu.VMEM((keys, head_dim), jnp.bfloat16),
                pltpu.VMEM((keys, head_dim), jnp.bfloat16),
                pltpu.VMEM((keys, head_dim), jnp.bfloat16),
                pltpu.VMEM((head_dim, keys), jnp.bfloat16),
                pltpu.VMEM((keys, head_dim), jnp.float32),
                pltpu.VMEM((keys, head_dim), jnp.float32),
            ],
        ),
        out_shape=[jax.ShapeDtypeStruct((tokens, group_width), jnp.bfloat16)] * 4
        + [jax.ShapeDtypeStruct((tile, width), jnp.bfloat16)] * 8,
        name="attend",
    )(table, *tiles, own_query, *queries, own_cotangent, *cotangents, q_gain, k_gain, row_live)


def collect_kernel(tile, slots, table_ref, *refs):
    parts, out = refs[:-1], refs[-1]
    for slot in range(slots):
        origin = table_ref[slot]
        rows = slice(slot * tile, (slot + 1) * tile)

        @pl.when(origin >= len(parts))
        def _():
            out[rows, :] = jnp.zeros((tile, out.shape[1]), out.dtype)

        for index in range(len(parts)):

            @pl.when(origin == index)
            def _():
                out[rows, :] = parts[index][...]


def collect(table, parts, slots):
    tile, width = parts[0].shape
    return pl.pallas_call(
        functools.partial(collect_kernel, tile, slots),
        grid_spec=pltpu.PrefetchScalarGridSpec(
            num_scalar_prefetch=1,
            grid=(1,),
            in_specs=[whole((tile, width))] * len(parts),
            out_specs=whole((slots * tile, width)),
        ),
        out_shape=jax.ShapeDtypeStruct((slots * tile, width), jnp.bfloat16),
        name="collect",
    )(table, *parts)


def head_device(
    images,
    kv_weight,
    q_gain,
    k_gain,
    queries,
    cotangent,
    tile_count,
    tile_target,
    tile_source,
    text_length,
):
    n_doc, n_seq = 8, 4
    doc_at = lax.axis_index("doc")
    seq_at = lax.axis_index("seq")
    slots, tile = images.shape[1], images.shape[2]
    rows_each = kv_weight.shape[0]
    tokens = queries.shape[1]
    group_width = queries.shape[2] // n_seq
    own_cols = images[0].reshape(slots * tile, images.shape[3])

    def group_of(value, step):
        return lax.dynamic_slice_in_dim(value[0], (seq_at ^ step) * group_width, group_width, 1)

    query_in = [swap_seq(group_of(queries, step), step) for step in (1, 2, 3)]
    other_cols = swap_doc(own_cols, 1)

    half = rows_each // 2
    weight = {0: kv_weight}
    weight[2] = swap_doc(kv_weight, 2)
    weight[4] = swap_doc(kv_weight, 4)
    weight[1] = swap_doc(kv_weight, 1)
    weight[3] = swap_doc(weight[2], 1)
    weight[6] = jnp.concatenate(
        [swap_doc(weight[4][:half], 2), swap_doc(weight[2][half:], 4)], axis=0
    )
    weight[5] = swap_doc(weight[4], 1)
    weight[7] = swap_doc(weight[6], 1)

    def project(steps):
        stacked = jnp.concatenate([weight[step] for step in steps], axis=0)
        part = lax.dot_general(
            own_cols, stacked, (((1,), (1,)), ((), ())), preferred_element_type=jnp.float32
        ).astype(jnp.bfloat16)
        parts = []
        for step in range(n_seq):
            block = (doc_at % n_seq) ^ seq_at ^ step
            piece = lax.dynamic_slice_in_dim(part, block * rows_each, rows_each, 1)
            parts.append(swap_seq(piece, step) if step else piece)
        return parts

    first = project((0, 1, 2, 3))
    second = project((4, 5, 6, 7))
    cot_in = [swap_seq(group_of(cotangent, step), step) for step in (1, 2, 3)]

    targets = tile_target[doc_at]
    sources = tile_source[doc_at]
    tiles_here = tile_count[doc_at]
    steps = jnp.arange(n_doc, dtype=jnp.int32)
    sent_slot = jnp.argmax(targets[None, :] == (steps ^ doc_at)[:, None], axis=1).astype(jnp.int32)
    send_table = jnp.concatenate([(doc_at // n_seq).astype(jnp.int32)[None], sent_slot])
    sent = dispatch(send_table, first, second, tile, n_doc)
    tiles = [sent[0]] + [swap_doc(sent[step], step) for step in range(1, n_doc)]

    attend_table = jnp.concatenate(
        [seq_at.astype(jnp.int32)[None], tiles_here[None], sources ^ doc_at]
    )
    row_index = jnp.concatenate(
        [(seq_at ^ step) * tokens + jnp.arange(tokens, dtype=jnp.int32) for step in range(n_seq)]
    )
    row_live = (row_index < text_length[doc_at]).astype(jnp.float32)[None]
    results = attend_call(
        attend_table,
        tiles,
        queries,
        query_in,
        cotangent,
        cot_in,
        q_gain[None],
        k_gain[None],
        row_live,
        slots,
    )
    mixed, grads = results[:n_seq], results[n_seq:]

    back = [grads[0]] + [swap_doc(grads[step], step) for step in range(1, n_doc)]
    back_table = jnp.where(targets < n_doc, targets ^ doc_at, n_doc).astype(jnp.int32)
    grad_own = collect(back_table, back, slots)

    odd = (doc_at ^ seq_at) % 2
    partner = swap_some(grad_own, 1, 0, lambda doc, seq: (doc ^ seq) % 2 == 1)
    pair = jnp.concatenate([grad_own, partner], axis=0)
    moved = [
        swap_some(pair, 0, step, lambda doc, seq: (doc ^ seq) % 2 == 0) for step in (1, 2, 3)
    ]
    near = jnp.where(odd == 1, moved[0], pair)
    far = jnp.where(odd == 1, moved[2], moved[1])
    near_head = seq_at ^ odd
    both_cols = jnp.concatenate([own_cols, other_cols], axis=0)

    def block(x_step, y_step):
        head = (doc_at % n_seq) ^ (2 * x_step)
        chosen = jnp.where(head == near_head, near, far)
        side = (doc_at // n_seq) ^ y_step
        chosen = lax.dynamic_slice_in_dim(chosen, side * rows_each, rows_each, 1)
        return lax.dot_general(
            chosen, both_cols, (((0,), (0,)), ((), ())), preferred_element_type=jnp.float32
        )

    arrived = [
        swap_doc(block(x_step, y_step).astype(jnp.bfloat16), 2 * x_step + 4 * y_step)
        for x_step, y_step in ((1, 1), (1, 0), (0, 1))
    ]
    weight_grad = block(0, 0)
    for part in arrived:
        weight_grad = weight_grad + part.astype(jnp.float32)

    attn_out = jnp.zeros(queries.shape[1:], jnp.bfloat16)
    for step in range(n_seq):
        piece = swap_seq(mixed[step], step) if step else mixed[0]
        attn_out = lax.dynamic_update_slice_in_dim(
            attn_out, piece, (seq_at ^ step) * group_width, 1
        )
    return (attn_out[None], weight_grad)


def solution(mesh):
    by_heads = dict(mesh.shape) == {"doc": 8, "seq": 4}
    return jax.shard_map(
        head_device if by_heads else any_mesh_device,
        mesh=mesh,
        in_specs=(
            P("doc", None, None, "seq"),
            P("doc", "seq"),
            P(),
            P(),
            P("doc", "seq", None),
            P("doc", "seq", None),
            P(),
            P(),
            P(),
            P(),
        ),
        out_specs=(P("doc", "seq", None), P("doc", "seq")),
        check_vma=False,
    )
```

```python
import functools
import math

import jax
import jax.numpy as jnp
from jax import lax
from jax.experimental import pallas as pl
from jax.experimental.pallas import tpu as pltpu
from jax.sharding import PartitionSpec as P

EPS = 1e-05
LOG2E = 1.4426950408889634


def cross_core(kv_tiles, query_rows, grad_rows, q_gain, k_gain, key_live, row_live):
    key_width = kv_tiles.shape[-1] // 2
    head_dim = q_gain.shape[0]
    kv_heads = key_width // head_dim
    token_rows = query_rows.shape[0]
    q_heads = query_rows.shape[1] // head_dim
    group_size = q_heads // kv_heads
    inv_root = 1.0 / math.sqrt(head_dim)
    key_raw = kv_tiles[:, :key_width].reshape(-1, kv_heads, head_dim).astype(jnp.float32)
    values = kv_tiles[:, key_width:].reshape(-1, kv_heads, head_dim)
    key_scale = lax.rsqrt(jnp.mean(key_raw * key_raw, axis=-1, keepdims=True) + EPS)
    key_normed = (key_raw * key_scale * k_gain).astype(jnp.bfloat16)
    query_raw = query_rows.reshape(token_rows, kv_heads, group_size, head_dim).astype(jnp.float32)
    query_scale = lax.rsqrt(jnp.mean(query_raw * query_raw, axis=-1, keepdims=True) + EPS)
    query_normed = (query_raw * query_scale * q_gain).astype(jnp.bfloat16)
    row_mask = row_live[:, None, None, None]
    grad_live = grad_rows.reshape(token_rows, kv_heads, group_size, head_dim) * row_mask.astype(
        jnp.bfloat16
    )

    def one_head(items):
        key_head, value_head, query_head, grad_head = items
        scores = (
            jnp.einsum("tgd,ld->tgl", query_head, key_head, preferred_element_type=jnp.float32)
            * inv_root
        )
        expd = jnp.exp(scores) * key_live
        attend = expd / jnp.sum(expd, axis=-1, keepdims=True)
        attend_low = attend.astype(jnp.bfloat16)
        mixed = jnp.einsum(
            "tgl,ld->tgd", attend_low, value_head, preferred_element_type=jnp.float32
        )
        mixed_low = (mixed * row_live[:, None, None]).astype(jnp.bfloat16)
        grad_attend = jnp.einsum(
            "tgd,ld->tgl", grad_head, value_head, preferred_element_type=jnp.float32
        )
        grad_scores = attend * (grad_attend - jnp.sum(attend * grad_attend, axis=-1, keepdims=True))
        grad_low = (grad_scores * inv_root).astype(jnp.bfloat16)
        grad_keyn = jnp.einsum(
            "tgl,tgd->ld", grad_low, query_head, preferred_element_type=jnp.float32
        )
        grad_values = jnp.einsum(
            "tgl,tgd->ld", attend_low, grad_head, preferred_element_type=jnp.float32
        )
        return (mixed_low, grad_keyn, grad_values)

    head_items = (
        jnp.moveaxis(key_normed, 1, 0),
        jnp.moveaxis(values, 1, 0),
        jnp.moveaxis(query_normed, 1, 0),
        jnp.moveaxis(grad_live, 1, 0),
    )
    mixed_heads, keyn_heads, value_heads = lax.map(one_head, head_items)
    attn_rows = jnp.moveaxis(mixed_heads, 0, 1).reshape(token_rows, -1)
    grad_keyn = jnp.moveaxis(keyn_heads, 0, 1)
    grad_values = jnp.moveaxis(value_heads, 0, 1)
    weighted = grad_keyn * k_gain
    cubed = key_scale * key_scale * key_scale
    grad_keys = key_scale * weighted - key_raw * cubed * jnp.mean(
        weighted * key_raw, axis=-1, keepdims=True
    )
    grad_kv = jnp.concatenate(
        [grad_keys.reshape(-1, key_width), grad_values.reshape(-1, key_width)], axis=-1
    )
    return (attn_rows, grad_kv)


def any_mesh_device(
    images,
    kv_weight,
    q_gain,
    k_gain,
    queries,
    cotangent,
    tile_count,
    tile_target,
    tile_source,
    text_length,
):
    n_doc = lax.axis_size("doc")
    n_seq = lax.axis_size("seq")
    doc_at = lax.axis_index("doc")
    seq_at = lax.axis_index("seq")
    slots = images.shape[1]
    tile_rows = images.shape[2]
    part_rows = tile_rows // n_seq
    own_cols = images[0].reshape(slots * tile_rows, images.shape[3])
    partial_value = lax.dot_general(
        own_cols,
        lax.all_gather(kv_weight, "doc", axis=0, tiled=True),
        (((1,), (1,)), ((), ())),
        preferred_element_type=jnp.float32,
    )
    width = partial_value.shape[1]
    partial_value = partial_value.reshape(slots, tile_rows, width)
    summed = lax.psum(partial_value.astype(jnp.bfloat16), "seq").astype(jnp.float32)
    own_share = lax.dynamic_slice_in_dim(summed, seq_at * part_rows, part_rows, 1)
    kv_own = own_share.astype(jnp.bfloat16)
    doc_ids = jnp.arange(n_doc, dtype=jnp.int32)
    slot_ids = jnp.arange(slots, dtype=jnp.int32)
    targets = tile_target[doc_at]
    send_map = (targets[None, :] == doc_ids[:, None]).astype(jnp.bfloat16)
    outgoing = jnp.einsum(
        "ds,src->drc", send_map, kv_own, preferred_element_type=jnp.float32
    ).astype(jnp.bfloat16)
    incoming = lax.all_to_all(outgoing, "doc", split_axis=0, concat_axis=0, tiled=True)
    tiles_here = tile_count[doc_at]
    sources = tile_source[doc_at]
    live_slot = slot_ids < tiles_here
    pick_map = ((sources[:, None] == doc_ids[None, :]) & live_slot[:, None]).astype(jnp.bfloat16)
    kv_part = jnp.einsum(
        "se,erc->src", pick_map, incoming, preferred_element_type=jnp.float32
    ).astype(jnp.bfloat16)
    kv_full = lax.all_gather(kv_part, "seq", axis=1, tiled=True)
    token_rows = queries.shape[1]
    key_live = (jnp.arange(slots * tile_rows, dtype=jnp.int32) // tile_rows < tiles_here).astype(
        jnp.float32
    )
    row_index = seq_at * token_rows + jnp.arange(token_rows, dtype=jnp.int32)
    row_live = (row_index < text_length[doc_at]).astype(jnp.float32)
    attn_rows, grad_kv = cross_core(
        kv_full.reshape(slots * tile_rows, width),
        queries[0],
        cotangent[0],
        q_gain,
        k_gain,
        key_live,
        row_live,
    )
    attn_out = attn_rows[None]
    grad_kv = grad_kv.reshape(slots, tile_rows, width)
    grad_sum = lax.psum(grad_kv.astype(jnp.bfloat16), "seq").astype(jnp.float32)
    grad_share = lax.dynamic_slice_in_dim(grad_sum, seq_at * part_rows, part_rows, 1)
    grad_own = grad_share.astype(jnp.bfloat16)
    back_out = jnp.einsum(
        "se,src->erc", pick_map, grad_own, preferred_element_type=jnp.float32
    ).astype(jnp.bfloat16)
    back_in = lax.all_to_all(back_out, "doc", split_axis=0, concat_axis=0, tiled=True)
    returned = jnp.einsum(
        "ds,drc->src", send_map, back_in, preferred_element_type=jnp.float32
    ).astype(jnp.bfloat16)
    grad_full = lax.all_gather(returned, "seq", axis=1, tiled=True)
    grad_flat = grad_full.reshape(slots * tile_rows, width)
    rows_each = width // n_doc
    weight_part = lax.dot_general(
        grad_flat, own_cols, (((0,), (0,)), ((), ())), preferred_element_type=jnp.float32
    )
    weight_sum = lax.psum(weight_part.astype(jnp.bfloat16), "doc").astype(jnp.float32)
    weight_grad = lax.dynamic_slice_in_dim(weight_sum, doc_at * rows_each, rows_each, 0)
    return (attn_out, weight_grad)


def swap_doc(value, step):
    pairs = [(at, at ^ step) for at in range(lax.axis_size("doc"))]
    return lax.ppermute(value, "doc", pairs)


def swap_seq(value, step):
    pairs = [(at, at ^ step) for at in range(lax.axis_size("seq"))]
    return lax.ppermute(value, "seq", pairs)


def swap_some(value, doc_step, seq_step, keep):
    n_doc = lax.axis_size("doc")
    n_seq = lax.axis_size("seq")
    pairs = [
        (doc * n_seq + seq, (doc ^ doc_step) * n_seq + (seq ^ seq_step))
        for doc in range(n_doc)
        for seq in range(n_seq)
        if keep(doc, seq)
    ]
    return lax.ppermute(value, ("doc", "seq"), pairs)


def whole(shape):
    return pl.BlockSpec(shape, lambda *_: (0,) * len(shape))


def dispatch_kernel(tile, table_ref, *refs):
    first, second = refs[:4], refs[4:8]
    outs, both = refs[8:-1], refs[-1]
    width = first[0].shape[1]

    def total(parts):
        value = parts[0][...].astype(jnp.float32)
        for part in parts[1:]:
            value = value + part[...].astype(jnp.float32)
        return value.astype(jnp.bfloat16)

    keys_first = table_ref[0] == 0

    @pl.when(keys_first)
    def _():
        both[:, :width] = total(first)
        both[:, width:] = total(second)

    @pl.when(jnp.logical_not(keys_first))
    def _():
        both[:, :width] = total(second)
        both[:, width:] = total(first)

    for step, out in enumerate(outs):
        slot = table_ref[1 + step]
        out[...] = both[pl.ds(pl.multiple_of(slot * tile, tile), tile), :]


def dispatch(table, first, second, tile, n_doc):
    rows, width = first[0].shape
    return pl.pallas_call(
        functools.partial(dispatch_kernel, tile),
        in_specs=[pl.BlockSpec(memory_space=pltpu.SMEM)]
        + [pl.BlockSpec(memory_space=pltpu.VMEM)] * 8,
        out_specs=[pl.BlockSpec(memory_space=pltpu.VMEM)] * n_doc,
        scratch_shapes=[pltpu.VMEM((rows, 2 * width), jnp.bfloat16)],
        out_shape=[jax.ShapeDtypeStruct((tile, 2 * width), jnp.bfloat16)] * n_doc,
        name="dispatch",
    )(table, *first, *second)


def forward_kernel(slots, table_ref, *refs):
    tiles, queries = refs[:8], refs[8:12]
    q_gain, k_gain, row_live = refs[12:15]
    outs = refs[15:19]
    attends, query_out, key_raw, values = refs[19:23]
    key_norm, values_t = refs[23:]
    tile, head_dim = tiles[0].shape[0], key_raw.shape[1]
    inv_root = 1.0 / math.sqrt(head_dim)
    count = table_ref[1]

    def slot_rows(slot):
        return slice(slot * tile, (slot + 1) * tile)

    @pl.when(pl.program_id(0) == 0)
    def _():
        for slot in range(slots):
            live = slot < count
            origin = table_ref[2 + slot]

            @pl.when(jnp.logical_not(live))
            def _():
                key_raw[slot_rows(slot), :] = jnp.zeros((tile, head_dim), jnp.bfloat16)
                values[slot_rows(slot), :] = jnp.zeros((tile, head_dim), jnp.bfloat16)

            for index in range(8):

                @pl.when(jnp.logical_and(live, origin == index))
                def _():
                    key_raw[slot_rows(slot), :] = tiles[index][:, :head_dim]
                    values[slot_rows(slot), :] = tiles[index][:, head_dim:]

        raw = key_raw[...].astype(jnp.float32)
        scale = lax.rsqrt(jnp.mean(raw * raw, axis=-1, keepdims=True) + EPS)
        key_norm[...] = (raw * scale * k_gain[...]).astype(jnp.bfloat16)
        values_t[...] = values[...].astype(jnp.float32).T.astype(jnp.bfloat16)

    for half in range(2):
        lanes = slice(2 * half * tile, 2 * (half + 1) * tile)
        raw = jnp.concatenate(
            [queries[2 * half][...], queries[2 * half + 1][...]], axis=0
        ).astype(jnp.float32)
        scale = lax.rsqrt(jnp.mean(raw * raw, axis=-1, keepdims=True) + EPS)
        query = (raw * scale * q_gain[...]).astype(jnp.bfloat16)
        query_out[lanes, :] = query
        scores = lax.dot_general(
            key_norm[...], query, (((1,), (1,)), ((), ())), preferred_element_type=jnp.float32
        )
        expd = jnp.exp2(scores * (inv_root * LOG2E))
        total = jnp.zeros((1, expd.shape[1]), jnp.float32)
        for slot in range(slots):
            part = jnp.sum(expd[slot_rows(slot), :], axis=0, keepdims=True)
            total = total + jnp.where(slot < count, part, 0.0)
        attend_low = (expd * (row_live[:, lanes] / total)).astype(jnp.bfloat16)
        attends[:, lanes] = attend_low
        mixed = jnp.dot(values_t[...], attend_low, preferred_element_type=jnp.float32).T
        outs[2 * half][...] = mixed[:tile].astype(jnp.bfloat16)
        outs[2 * half + 1][...] = mixed[tile:].astype(jnp.bfloat16)


def forward_call(table, tiles, own_query, queries, q_gain, k_gain, row_live, slots):
    tile, width = tiles[0].shape
    head_dim = width // 2
    tokens, group_width = queries[0].shape
    group = group_width // head_dim
    keys, rows = slots * tile, 4 * tokens
    own = pl.BlockSpec((None, tokens, head_dim), lambda at, table: (0, 0, table[0] * group + at))
    moved = pl.BlockSpec((tokens, head_dim), lambda at, table: (0, at))

    def by_head(shape):
        return pl.BlockSpec((None,) + shape, lambda at, table: (at, 0, 0))

    return pl.pallas_call(
        functools.partial(forward_kernel, slots),
        grid_spec=pltpu.PrefetchScalarGridSpec(
            num_scalar_prefetch=1,
            grid=(group,),
            in_specs=[whole((tile, width))] * 8
            + [own] + [moved] * 3
            + [whole((1, head_dim)), whole((1, head_dim)), whole((1, rows))],
            out_specs=[moved] * 4
            + [by_head((keys, rows)), by_head((rows, head_dim))]
            + [whole((keys, head_dim))] * 2,
            scratch_shapes=[
                pltpu.VMEM((keys, head_dim), jnp.bfloat16),
                pltpu.VMEM((head_dim, keys), jnp.bfloat16),
            ],
        ),
        out_shape=[jax.ShapeDtypeStruct((tokens, group_width), jnp.bfloat16)] * 4
        + [
            jax.ShapeDtypeStruct((group, keys, rows), jnp.bfloat16),
            jax.ShapeDtypeStruct((group, rows, head_dim), jnp.bfloat16),
        ]
        + [jax.ShapeDtypeStruct((keys, head_dim), jnp.bfloat16)] * 2,
        name="forward",
    )(table, *tiles, own_query, *queries, q_gain, k_gain, row_live)


def backward_kernel(slots, steps, table_ref, *refs):
    cotangents = refs[:4]
    attends, query_in, key_raw, values, k_gain = refs[4:9]
    grads = refs[9:17]
    grad_k, grad_v, both = refs[17:]
    tile, head_dim = cotangents[0].shape[0], key_raw.shape[1]
    inv_root = 1.0 / math.sqrt(head_dim)
    step = pl.program_id(0)
    count = table_ref[1]

    def slot_rows(slot):
        return slice(slot * tile, (slot + 1) * tile)

    @pl.when(step == 0)
    def _():
        grad_k[...] = jnp.zeros_like(grad_k)
        grad_v[...] = jnp.zeros_like(grad_v)

    for half in range(2):
        lanes = slice(2 * half * tile, 2 * (half + 1) * tile)
        grad_in = jnp.concatenate([cotangents[2 * half][...], cotangents[2 * half + 1][...]], axis=0)
        attend_low = attends[:, lanes]
        attend = attend_low.astype(jnp.float32)
        grad_attend = lax.dot_general(
            values[...], grad_in, (((1,), (1,)), ((), ())), preferred_element_type=jnp.float32
        )
        product = attend * grad_attend
        shift = jnp.sum(product, axis=0, keepdims=True)
        grad_low = ((product - attend * shift) * inv_root).astype(jnp.bfloat16)
        grad_k[...] += jnp.dot(grad_low, query_in[lanes, :], preferred_element_type=jnp.float32)
        grad_v[...] += jnp.dot(attend_low, grad_in, preferred_element_type=jnp.float32)

    @pl.when(step == steps - 1)
    def _():
        raw = key_raw[...].astype(jnp.float32)
        scale = lax.rsqrt(jnp.mean(raw * raw, axis=-1, keepdims=True) + EPS)
        weighted = grad_k[...] * k_gain[...]
        cubed = scale * scale * scale
        grad_raw = scale * weighted - raw * cubed * jnp.mean(
            weighted * raw, axis=-1, keepdims=True
        )
        both[:, :head_dim] = grad_raw.astype(jnp.bfloat16)
        both[:, head_dim:] = grad_v[...].astype(jnp.bfloat16)
        for grad in grads:
            grad[...] = jnp.zeros_like(grad)
        for slot in range(slots):
            live = slot < count
            origin = table_ref[2 + slot]
            for index in range(8):

                @pl.when(jnp.logical_and(live, origin == index))
                def _():
                    grads[index][...] = both[slot_rows(slot), :]


def backward_call(table, own_cotangent, cotangents, attends, query_in, key_raw, values, k_gain, slots):
    tokens, group_width = cotangents[0].shape
    group, keys, rows = attends.shape
    head_dim = key_raw.shape[1]
    tile = keys // slots
    own = pl.BlockSpec((None, tokens, head_dim), lambda at, table: (0, 0, table[0] * group + at))
    moved = pl.BlockSpec((tokens, head_dim), lambda at, table: (0, at))

    def by_head(shape):
        return pl.BlockSpec((None,) + shape, lambda at, table: (at, 0, 0))

    return pl.pallas_call(
        functools.partial(backward_kernel, slots, group),
        grid_spec=pltpu.PrefetchScalarGridSpec(
            num_scalar_prefetch=1,
            grid=(group,),
            in_specs=[own] + [moved] * 3
            + [by_head((keys, rows)), by_head((rows, head_dim))]
            + [whole((keys, head_dim))] * 2
            + [whole((1, head_dim))],
            out_specs=[whole((tile, 2 * head_dim))] * 8,
            scratch_shapes=[
                pltpu.VMEM((keys, head_dim), jnp.float32),
                pltpu.VMEM((keys, head_dim), jnp.float32),
                pltpu.VMEM((keys, 2 * head_dim), jnp.bfloat16),
            ],
        ),
        out_shape=[jax.ShapeDtypeStruct((tile, 2 * head_dim), jnp.bfloat16)] * 8,
        name="backward",
    )(table, own_cotangent, *cotangents, attends, query_in, key_raw, values, k_gain)


def collect_kernel(tile, slots, table_ref, *refs):
    parts, out = refs[:-1], refs[-1]
    for slot in range(slots):
        origin = table_ref[slot]
        rows = slice(slot * tile, (slot + 1) * tile)

        @pl.when(origin >= len(parts))
        def _():
            out[rows, :] = jnp.zeros((tile, out.shape[1]), out.dtype)

        for index in range(len(parts)):

            @pl.when(origin == index)
            def _():
                out[rows, :] = parts[index][...]


def collect(table, parts, slots):
    tile, width = parts[0].shape
    return pl.pallas_call(
        functools.partial(collect_kernel, tile, slots),
        in_specs=[pl.BlockSpec(memory_space=pltpu.SMEM)]
        + [pl.BlockSpec(memory_space=pltpu.VMEM)] * len(parts),
        out_specs=pl.BlockSpec(memory_space=pltpu.VMEM),
        out_shape=jax.ShapeDtypeStruct((slots * tile, width), jnp.bfloat16),
        name="collect",
    )(table, *parts)


def head_device(
    images,
    kv_weight,
    q_gain,
    k_gain,
    queries,
    cotangent,
    tile_count,
    tile_target,
    tile_source,
    text_length,
):
    n_doc, n_seq = 8, 4
    doc_at = lax.axis_index("doc")
    seq_at = lax.axis_index("seq")
    slots, tile = images.shape[1], images.shape[2]
    rows_each = kv_weight.shape[0]
    tokens = queries.shape[1]
    group_width = queries.shape[2] // n_seq
    own_cols = images[0].reshape(slots * tile, images.shape[3])

    def group_of(value, step):
        return lax.dynamic_slice_in_dim(value[0], (seq_at ^ step) * group_width, group_width, 1)

    query_in = [swap_seq(group_of(queries, step), step) for step in (1, 2, 3)]
    other_cols = swap_doc(own_cols, 1)

    half = rows_each // 2
    weight = {0: kv_weight}
    weight[2] = swap_doc(kv_weight, 2)
    weight[4] = swap_doc(kv_weight, 4)
    weight[1] = swap_doc(kv_weight, 1)
    weight[3] = swap_doc(weight[2], 1)
    weight[6] = jnp.concatenate(
        [swap_doc(weight[4][:half], 2), swap_doc(weight[2][half:], 4)], axis=0
    )
    weight[5] = swap_doc(weight[4], 1)
    weight[7] = swap_doc(weight[6], 1)

    def project(steps):
        stacked = jnp.concatenate([weight[step] for step in steps], axis=0)
        part = lax.dot_general(
            own_cols, stacked, (((1,), (1,)), ((), ())), preferred_element_type=jnp.float32
        ).astype(jnp.bfloat16)
        parts = []
        for step in range(n_seq):
            block = (doc_at % n_seq) ^ seq_at ^ step
            piece = lax.dynamic_slice_in_dim(part, block * rows_each, rows_each, 1)
            parts.append(swap_seq(piece, step) if step else piece)
        return parts

    first = project((0, 1, 2, 3))
    second = project((4, 5, 6, 7))
    cot_out = [group_of(cotangent, step) for step in (1, 2, 3)]
    first, second, cot_out = lax.optimization_barrier((first, second, cot_out))
    cot_in = [swap_seq(value, step) for step, value in zip((1, 2, 3), cot_out)]

    targets = tile_target[doc_at]
    sources = tile_source[doc_at]
    tiles_here = tile_count[doc_at]
    steps = jnp.arange(n_doc, dtype=jnp.int32)
    sent_slot = jnp.argmax(targets[None, :] == (steps ^ doc_at)[:, None], axis=1).astype(jnp.int32)
    send_table = jnp.concatenate([(doc_at // n_seq).astype(jnp.int32)[None], sent_slot])
    sent = dispatch(send_table, first, second, tile, n_doc)
    tiles = [sent[0]] + [swap_doc(sent[step], step) for step in range(1, n_doc)]

    attend_table = jnp.concatenate(
        [seq_at.astype(jnp.int32)[None], tiles_here[None], sources ^ doc_at]
    )
    row_index = jnp.concatenate(
        [(seq_at ^ step) * tokens + jnp.arange(tokens, dtype=jnp.int32) for step in range(n_seq)]
    )
    row_live = (row_index < text_length[doc_at]).astype(jnp.float32)[None]
    results = forward_call(
        attend_table, tiles, queries, query_in, q_gain[None], k_gain[None], row_live, slots
    )
    mixed = results[:n_seq]
    attends, query_normed, key_raw, values = results[n_seq:]
    grads = backward_call(
        attend_table, cotangent, cot_in, attends, query_normed, key_raw, values, k_gain[None], slots
    )

    back = [grads[0]] + [swap_doc(grads[step], step) for step in range(1, n_doc)]
    back_table = jnp.where(targets < n_doc, targets ^ doc_at, n_doc).astype(jnp.int32)
    grad_own = collect(back_table, back, slots)

    odd = (doc_at ^ seq_at) % 2
    partner = swap_some(grad_own, 1, 0, lambda doc, seq: (doc ^ seq) % 2 == 1)
    pair = jnp.concatenate([grad_own, partner], axis=0)
    moved = [
        swap_some(pair, 0, step, lambda doc, seq: (doc ^ seq) % 2 == 0) for step in (1, 2, 3)
    ]
    moved, mixed = lax.optimization_barrier((moved, mixed))
    near = jnp.where(odd == 1, moved[0], pair)
    far = jnp.where(odd == 1, moved[2], moved[1])
    near_head = seq_at ^ odd
    both_cols = jnp.concatenate([own_cols, other_cols], axis=0)

    def block(x_step, y_step):
        head = (doc_at % n_seq) ^ (2 * x_step)
        chosen = jnp.where(head == near_head, near, far)
        side = (doc_at // n_seq) ^ y_step
        chosen = lax.dynamic_slice_in_dim(chosen, side * rows_each, rows_each, 1)
        return lax.dot_general(
            chosen, both_cols, (((0,), (0,)), ((), ())), preferred_element_type=jnp.float32
        )

    arrived = [
        swap_doc(block(x_step, y_step).astype(jnp.bfloat16), 2 * x_step + 4 * y_step)
        for x_step, y_step in ((1, 1), (1, 0), (0, 1))
    ]
    weight_grad = lax.optimization_barrier(block(0, 0))
    for part in arrived:
        weight_grad = weight_grad + part.astype(jnp.float32)

    attn_out = jnp.zeros(queries.shape[1:], jnp.bfloat16)
    for step in range(n_seq):
        piece = swap_seq(mixed[step], step) if step else mixed[0]
        attn_out = lax.dynamic_update_slice_in_dim(
            attn_out, piece, (seq_at ^ step) * group_width, 1
        )
    return (attn_out[None], weight_grad)


def solution(mesh):
    by_heads = dict(mesh.shape) == {"doc": 8, "seq": 4}
    return jax.shard_map(
        head_device if by_heads else any_mesh_device,
        mesh=mesh,
        in_specs=(
            P("doc", None, None, "seq"),
            P("doc", "seq"),
            P(),
            P(),
            P("doc", "seq", None),
            P("doc", "seq", None),
            P(),
            P(),
            P(),
            P(),
        ),
        out_specs=(P("doc", "seq", None), P("doc", "seq")),
        check_vma=False,
    )
```
